32 devices in a mesh: groups: 2 (over x), lbond: 16 (over z, y, core).
Axes of the slice: x: 2, y: 2, z: 4, core: 2. Of those that a mesh axis runs over, the one named last changes fastest.
Arguments:
- env_in: bfloat16 [4096, 1024], P('lbond', 'groups'), parts along dimension 1, may hold values from -6 to 6
- site_tensors: bfloat16 [4, 4096, 4, 4096], P(None, 'lbond'), may hold values from -0.125 to 0.125
- weight_table: float32 [64, 4], replicated, may hold values from -3 to 3
- state_codes: int32 [4, 1024], P(None, 'groups'), parts along dimension 1, may hold values from 0 to 63
- rescale: int32 [4], replicated, may hold values from 1 to 3
Outputs:
- env_out: bfloat16 [4096, 1024], P('lbond', 'groups'), parts along dimension 1
The draws below stay inside these ranges and needn't reach their ends.
There are 2 independent parts, one for each index of `groups`. The reference program is written for one: setup_inputs(seed, part) draws one part's arguments, and reference() takes and returns one part's arrays. A program takes and returns all parts, laid end to end along the dimension named above; an argument that names none is the same for every part. Nothing has to cross between parts.
All inputs are finite; a program needn't handle non-finite values.
Results may differ from the reference program's by a relative error of at most 0.018.
Values may be sent and summed in bfloat16 or wider, within the bound.
No kernel may reach another device: no remote copies, remote signals or barrier semaphores. Data moves between devices by JAX's collectives and lax.ppermute only.
A program may use at most 128 MiB of HBM per device.

```python
import jax
import jax.numpy as jnp

CHI = 4096
PHOT = 4
SITES = 4
TABLE = 64
ROWS = 512


def set_ends(array, key, low, top_value):
    shape = array.shape
    index_at = [jax.random.randint(jax.random.fold_in(key, axis), (), 0, shape[axis]) for axis in range(len(shape))]
    array = array.at[tuple(index_at)].set(low)
    longest = shape.index(max(shape))
    index_at[longest] = (index_at[longest] + 1) % shape[longest]
    return array.at[tuple(index_at)].set(top_value)


def with_spikes(result, key, source, target, shards_of, factor):
    owner, partner = [(jnp.arange(result.shape[axis_at]) // (result.shape[axis_at] // shards_of)).reshape([-1 if axis == axis_at else 1 for axis in range(result.ndim)]) for axis_at in (source, target)]
    chosen = jax.random.permutation(key, shards_of)[partner]
    strong = (owner == chosen) | (owner == (partner + shards_of // 2) % shards_of)
    return jnp.where(strong, factor * result, result)


def block_scale(stream_key, shape, split, smallest, top_value):
    gain = 1.0
    for axis_at, shards_of in split:
        draws = jax.random.uniform(jax.random.fold_in(jax.random.fold_in(stream_key, 6), axis_at), (shards_of,), jnp.float32, smallest / len(split), top_value / len(split))
        gain = gain * jnp.repeat(jnp.exp(draws), shape[axis_at] // shards_of).reshape((-1,) + (1,) * (len(shape) - 1 - axis_at))
    return gain


def noise(key, shape, scale, bound, pieces=(), held_as=jnp.bfloat16):
    entries = jax.random.normal(key, shape, jnp.float32) * scale
    if len(pieces) > 0:
        entries = block_scale(key, shape, pieces, -0.22, 0.18) * entries
    return jnp.clip(entries, min=-bound, max=bound).astype(held_as)


def noise_with(key, shape, width, reach, split, heavy, dtype=jnp.bfloat16):
    array = width * jax.random.normal(key, shape, jnp.float32)
    if split:
        array = array * block_scale(key, shape, split, -0.22, 0.18)
    return jnp.clip(with_spikes(array, jax.random.fold_in(key, 3), *heavy), -reach, reach).astype(dtype)


def setup_inputs(seed: int = 0, part: int = 0) -> dict:
    seeds = jax.random.split(jax.random.key(seed), 6)
    part_splits = jax.random.split(jax.random.fold_in(seeds[5], part), 6)
    env_in = noise(part_splits[0], (CHI, ROWS), 1.0, 6.0, ((0, 16),))
    site_tensors = noise_with(seeds[1], (SITES, CHI, PHOT, CHI), CHI ** -0.5, 0.125, ((1, 16),), (1, 3, 16, 2.0))
    weight_table = noise(seeds[2], (TABLE, PHOT), 0.5, 3.0, (), jnp.float32)
    state_codes = set_ends(jax.random.randint(part_splits[3], (SITES, ROWS), 0, TABLE), jax.random.fold_in(part_splits[3], 1), 0, TABLE - 1).astype(jnp.int32)
    rescale = set_ends(jax.random.randint(seeds[4], (SITES,), 1, 4), jax.random.fold_in(seeds[4], 1), 1, 3).astype(jnp.int32)
    return {"env_in": env_in, "site_tensors": site_tensors, "weight_table": weight_table, "state_codes": state_codes, "rescale": rescale}


def reference(env_in, site_tensors, weight_table, state_codes, rescale):
    weights = weight_table[state_codes]
    env = env_in
    for index in range(SITES):
        mix = jnp.transpose(weights[index])
        scaled = (env.astype(jnp.float32)[:, None, :] * mix[None, :, :]).astype(jnp.bfloat16)
        scaled = scaled.reshape(CHI * PHOT, ROWS)
        flat = site_tensors[index].reshape(CHI * PHOT, CHI)
        product = jnp.dot(flat.T, scaled, preferred_element_type=jnp.float32)
        factor = rescale[index].astype(jnp.float32) * 0.5
        env = (product * factor).astype(jnp.bfloat16)
    return env
```

```python
import functools

import jax
import jax.numpy as jnp
from jax import lax
from jax.experimental import pallas as pl
from jax.experimental.pallas import tpu as pltpu
from jax.sharding import PartitionSpec as P

LANES = 128
CHAINS = 2
VMEM_LIMIT = 24 << 20


def stage_masks(devices):
    masks = [1 << bit for bit in range(1, devices.bit_length() - 1)]
    swapped = masks[1::-1] + masks[2:]
    return masks, swapped


def relative(position, masks):
    offset = 0
    for step, mask in enumerate(masks):
        if (position >> (len(masks) - 1 - step)) & 1:
            offset ^= mask
    return offset


def chunk_owner(me, position, devices):
    even, odd = stage_masks(devices)
    half = devices // 2
    place = position % half
    parity = me % 2
    if position >= half:
        return me ^ 1 ^ jnp.where(parity == 1, relative(place, even), relative(place, odd))
    return me ^ jnp.where(parity == 1, relative(place, odd), relative(place, even))


def scaled_rows(env, codes, table, transposed):
    left = env.shape[0] if transposed else env.shape[1]
    photon = table.shape[1]
    depth = left * photon
    entries = table.shape[0]
    column = lax.broadcasted_iota(jnp.int32, (1, depth), 1)
    spread = (column // photon == lax.broadcasted_iota(jnp.int32, (left, 1), 0)).astype(jnp.bfloat16)
    dims = (((0,), (0,)), ((), ())) if transposed else (((1,), (0,)), ((), ()))
    repeated = lax.dot_general(env, spread, dims, preferred_element_type=jnp.float32)
    phase = column % photon
    wide = jnp.broadcast_to(table[:, :1], (entries, depth))
    for p in range(1, photon):
        wide = jnp.where(phase == p, table[:, p : p + 1], wide)
    parts = []
    for _ in range(3):
        part = wide.astype(jnp.bfloat16)
        parts.append(part)
        wide = wide - part.astype(jnp.float32)
    rows = codes.shape[1]
    hot = (codes == lax.broadcasted_iota(jnp.int32, (entries, rows), 0)).astype(jnp.bfloat16)
    weights = lax.dot_general(
        jnp.concatenate([hot] * 3, 0),
        jnp.concatenate(parts, 0),
        (((0,), (0,)), ((), ())),
        preferred_element_type=jnp.float32,
    )
    return (repeated * weights).astype(jnp.bfloat16)


def site_kernel(site, row0, devices, first, load, groups, *refs):
    me_ref, factor_ref, codes_ref, table_ref, *refs = refs
    terms, refs = refs[: 1 if first else devices.bit_length()], refs[1 if first else devices.bit_length() :]
    if load:
        tensors, send, keep, tiles, sems = refs
    else:
        tiles, send, keep = refs
    half = devices // 2
    width, photon = tiles.shape[1], tiles.shape[3]
    order = list(range(half, devices)) + list(range(half))
    me = me_ref[0]

    def copies(position):
        owner = chunk_owner(me, position, devices)
        for tile in range(width):
            start = pl.multiple_of((owner * width + tile) * LANES, LANES)
            yield pltpu.make_async_copy(
                tensors.at[site, :, :, pl.ds(start, LANES)], tiles.at[position, tile], sems.at[position]
            )

    if load:
        for position in order:
            for copy in copies(position):
                copy.start()
    rows = send.shape[1]
    if first:
        env = terms[0][:, row0 : row0 + rows]
    else:
        total = terms[0][...].astype(jnp.float32)
        for term in terms[1:]:
            total = total + term[...].astype(jnp.float32)
        env = (total * (factor_ref[site - 1].astype(jnp.float32) * 0.5)).astype(jnp.bfloat16)
    scaled = scaled_rows(env, codes_ref[site : site + 1, row0 : row0 + rows], table_ref[...], first)
    depth = tiles.shape[2] * photon
    done = 0
    for size in groups:
        batch = order[done : done + size]
        done += size
        if load:
            for position in batch:
                for copy in copies(position):
                    copy.wait()
        for position in batch:
            block = jnp.concatenate(
                [tiles.at[position, tile].reshape(depth, LANES)[...] for tile in range(width)], 1
            )
            product = jnp.dot(scaled, block, preferred_element_type=jnp.float32).astype(jnp.bfloat16)
            if position >= half:
                send[position - half] = product
            else:
                keep[position] = product


def group_sizes(devices):
    sizes = [devices // 4, devices // 4, devices // 4, devices // 8, devices // 8]
    return sizes


def site_call(site, row0, rows, devices, me, rescale, codes, table, terms, tensors, tiles):
    first = len(terms) == 1
    load = tiles is None
    _, left, photon, right = tensors.shape
    chunk = right // devices
    smem = pl.BlockSpec(memory_space=pltpu.SMEM)
    vmem = pl.BlockSpec(memory_space=pltpu.VMEM)
    if first:
        term_specs = [vmem]
    else:
        term_specs = [pl.BlockSpec((None, rows, chunk), lambda _: (0, 0, 0)) for _ in terms]
    piece = jax.ShapeDtypeStruct((devices // 2, rows, chunk), jnp.bfloat16)
    held = jax.ShapeDtypeStruct((devices, chunk // LANES, left, photon, LANES), tensors.dtype)
    groups = group_sizes(devices) if load else [devices]
    return pl.pallas_call(
        functools.partial(site_kernel, site, row0, devices, first, load, groups),
        grid=(1,),
        out_shape=[piece, piece] + ([held] if load else []),
        in_specs=[smem, smem, vmem, vmem] + term_specs + [pl.BlockSpec(memory_space=pl.ANY) if load else vmem],
        out_specs=[vmem, vmem] + ([vmem] if load else []),
        scratch_shapes=[pltpu.SemaphoreType.DMA((devices,))] if load else [],
        compiler_params=pltpu.CompilerParams(vmem_limit_bytes=VMEM_LIMIT),
        name=f"site{site}_rows{row0}",
    )(me, rescale, codes, table, *terms, tensors if load else tiles)


def exchange(value, stage, devices):
    even, odd = stage_masks(devices)
    pairs = [(i, i ^ ((odd if i & 1 else even)[stage] if stage >= 0 else 1)) for i in range(devices)]
    return lax.ppermute(value, "lbond", pairs)


def reduce_terms(send, keep, devices):
    terms = [keep, exchange(send, -1, devices)]
    blocks = devices // 2
    for stage in range(devices.bit_length() - 2):
        blocks //= 2
        total = terms[0][blocks : 2 * blocks].astype(jnp.float32)
        for term in terms[1:]:
            total = total + term[blocks : 2 * blocks].astype(jnp.float32)
        terms.append(exchange(total.astype(jnp.bfloat16), stage, devices))
    return terms


def on_device(devices, env_in, site_tensors, weight_table, state_codes, rescale):
    sites = site_tensors.shape[0]
    rows = env_in.shape[1] // CHAINS
    me = lax.axis_index("lbond").astype(jnp.int32).reshape(1)
    terms = [[env_in] for _ in range(CHAINS)]
    for site in range(sites):
        tiles = None
        for chain in range(CHAINS):
            made = site_call(
                site, chain * rows, rows, devices, me, rescale, state_codes, weight_table, terms[chain],
                site_tensors, tiles,
            )
            if tiles is None:
                tiles = made[2]
            terms[chain] = reduce_terms(made[0], made[1], devices)
    factor = rescale[sites - 1].astype(jnp.float32) * 0.5
    outs = []
    for chain in range(CHAINS):
        total = terms[chain][0][0].astype(jnp.float32)
        for term in terms[chain][1:]:
            total = total + term[0].astype(jnp.float32)
        outs.append((total * factor).astype(jnp.bfloat16).T)
    return jnp.concatenate(outs, 1)


def solution(mesh):
    placed = (P("lbond", "groups"), P(None, "lbond", None, None), P(), P(None, "groups"), P())
    return jax.shard_map(
        functools.partial(on_device, mesh.shape["lbond"]),
        mesh=mesh,
        in_specs=placed,
        out_specs=P("lbond", "groups"),
        check_vma=False,
    )
```

```python
import functools

import jax
import jax.numpy as jnp
from jax import lax
from jax.experimental import pallas as pl
from jax.experimental.pallas import tpu as pltpu
from jax.sharding import PartitionSpec as P

LANES = 128
SPLIT = (1, 1)
PRELOAD = True
VMEM_LIMIT = 24 << 20


def stage_masks(devices):
    masks = [1 << bit for bit in range(1, devices.bit_length() - 1)]
    swapped = masks[1::-1] + masks[2:]
    return masks, swapped


def relative(position, masks):
    offset = 0
    for step, mask in enumerate(masks):
        if (position >> (len(masks) - 1 - step)) & 1:
            offset ^= mask
    return offset


def chunk_owner(me, position, devices):
    even, odd = stage_masks(devices)
    half = devices // 2
    place = position % half
    parity = me % 2
    if position >= half:
        return me ^ 1 ^ jnp.where(parity == 1, relative(place, even), relative(place, odd))
    return me ^ jnp.where(parity == 1, relative(place, odd), relative(place, even))


def scaled_rows(env, codes, table, transposed):
    left = env.shape[0] if transposed else env.shape[1]
    photon, entries = table.shape
    depth = left * photon
    column = lax.broadcasted_iota(jnp.int32, (1, depth), 1)
    spread = (column // photon == lax.broadcasted_iota(jnp.int32, (left, 1), 0)).astype(jnp.bfloat16)
    dims = (((0,), (0,)), ((), ())) if transposed else (((1,), (0,)), ((), ()))
    repeated = lax.dot_general(env, spread, dims, preferred_element_type=jnp.float32)
    phase = (column % photon == lax.broadcasted_iota(jnp.int32, (photon, 1), 0)).astype(jnp.bfloat16)
    parts = []
    for _ in range(3):
        part = table.astype(jnp.bfloat16)
        table = table - part.astype(jnp.float32)
        wide = lax.dot_general(part, phase, (((0,), (0,)), ((), ())), preferred_element_type=jnp.float32)
        parts.append(wide.astype(jnp.bfloat16))
    rows = codes.shape[1]
    hot = (codes == lax.broadcasted_iota(jnp.int32, (entries, rows), 0)).astype(jnp.bfloat16)
    weights = lax.dot_general(
        jnp.concatenate([hot] * 3, 0),
        jnp.concatenate(parts, 0),
        (((0,), (0,)), ((), ())),
        preferred_element_type=jnp.float32,
    )
    return (repeated * weights).astype(jnp.bfloat16)


def site_kernel(site, row0, devices, first, load, groups, *refs):
    me_ref, factor_ref, codes_ref, table_ref, *refs = refs
    terms, refs = refs[: 1 if first else devices.bit_length()], refs[1 if first else devices.bit_length() :]
    if load:
        tensors, send, keep, tiles, sems = refs
    else:
        tiles, send, keep = refs
    half = devices // 2
    width, photon = tiles.shape[1], tiles.shape[3]
    order = list(range(half, devices)) + list(range(half))
    me = me_ref[0]

    def copies(position):
        owner = chunk_owner(me, position, devices)
        for tile in range(width):
            start = pl.multiple_of((owner * width + tile) * LANES, LANES)
            yield pltpu.make_async_copy(
                tensors.at[site, :, :, pl.ds(start, LANES)], tiles.at[position, tile], sems.at[position]
            )

    if load:
        for position in order:
            for copy in copies(position):
                copy.start()
    rows = send.shape[1]
    if first:
        env = terms[0][:, row0 : row0 + rows]
    else:
        total = terms[0][...].astype(jnp.float32)
        for term in terms[1:]:
            total = total + term[...].astype(jnp.float32)
        env = (total * (factor_ref[site - 1].astype(jnp.float32) * 0.5)).astype(jnp.bfloat16)
    scaled = scaled_rows(env, codes_ref[site : site + 1, row0 : row0 + rows], table_ref[...], first)
    depth = tiles.shape[2] * photon
    done = 0
    for size in groups:
        batch = order[done : done + size]
        done += size
        if load:
            for position in batch:
                for copy in copies(position):
                    copy.wait()
        for position in batch:
            block = jnp.concatenate(
                [tiles.at[position, tile].reshape(depth, LANES)[...] for tile in range(width)], 1
            )
            product = jnp.dot(scaled, block, preferred_element_type=jnp.float32).astype(jnp.bfloat16)
            if position >= half:
                send[position - half] = product
            else:
                keep[position] = product


def load_kernel(site, devices, me_ref, tensors, tiles, sems):
    width = tiles.shape[1]
    me = me_ref[0]
    copies = []
    for position in range(devices):
        owner = chunk_owner(me, position, devices)
        for tile in range(width):
            start = pl.multiple_of((owner * width + tile) * LANES, LANES)
            copies.append(
                pltpu.make_async_copy(
                    tensors.at[site, :, :, pl.ds(start, LANES)], tiles.at[position, tile], sems.at[position, tile]
                )
            )
    for copy in copies:
        copy.start()
    for copy in copies:
        copy.wait()


def load_call(site, devices, me, tensors):
    _, left, photon, right = tensors.shape
    width = right // devices // LANES
    return pl.pallas_call(
        functools.partial(load_kernel, site, devices),
        out_shape=jax.ShapeDtypeStruct((devices, width, left, photon, LANES), tensors.dtype),
        in_specs=[pl.BlockSpec(memory_space=pltpu.SMEM), pl.BlockSpec(memory_space=pl.ANY)],
        out_specs=pl.BlockSpec(memory_space=pltpu.VMEM),
        scratch_shapes=[pltpu.SemaphoreType.DMA((devices, width))],
        compiler_params=pltpu.CompilerParams(vmem_limit_bytes=VMEM_LIMIT),
    )(me, tensors)


def group_sizes(devices):
    sizes = [devices // 4, devices // 4, devices // 4, devices // 8, devices // 8]
    return sizes


def site_call(site, row0, rows, devices, me, rescale, codes, table, terms, tensors, tiles):
    first = len(terms) == 1
    load = tiles is None
    _, left, photon, right = tensors.shape
    chunk = right // devices
    smem = pl.BlockSpec(memory_space=pltpu.SMEM)
    vmem = pl.BlockSpec(memory_space=pltpu.VMEM)
    if first:
        term_specs = [vmem]
    else:
        term_specs = [pl.BlockSpec((None, rows, chunk), lambda _: (0, 0, 0)) for _ in terms]
    piece = jax.ShapeDtypeStruct((devices // 2, rows, chunk), jnp.bfloat16)
    held = jax.ShapeDtypeStruct((devices, chunk // LANES, left, photon, LANES), tensors.dtype)
    groups = group_sizes(devices) if load else [devices]
    return pl.pallas_call(
        functools.partial(site_kernel, site, row0, devices, first, load, groups),
        grid=(1,),
        out_shape=[piece, piece] + ([held] if load else []),
        in_specs=[smem, smem, vmem, vmem] + term_specs + [pl.BlockSpec(memory_space=pl.ANY) if load else vmem],
        out_specs=[vmem, vmem] + ([vmem] if load else []),
        scratch_shapes=[pltpu.SemaphoreType.DMA((devices,))] if load else [],
        compiler_params=pltpu.CompilerParams(vmem_limit_bytes=VMEM_LIMIT),
    )(me, rescale, codes, table, *terms, tensors if load else tiles)


def exchange(value, stage, devices):
    even, odd = stage_masks(devices)
    pairs = [(i, i ^ ((odd if i & 1 else even)[stage] if stage >= 0 else 1)) for i in range(devices)]
    return lax.ppermute(value, "lbond", pairs)


def reduce_terms(send, keep, devices):
    terms = [keep, exchange(send, -1, devices)]
    blocks = devices // 2
    for stage in range(devices.bit_length() - 2):
        blocks //= 2
        total = terms[0][blocks : 2 * blocks].astype(jnp.float32)
        for term in terms[1:]:
            total = total + term[blocks : 2 * blocks].astype(jnp.float32)
        total = total.astype(jnp.bfloat16)
        terms.append(exchange(total, stage, devices))
    return terms


def on_device(devices, *args):
    return chain_of_sites(devices, *args)


def chain_of_sites(devices, env_in, site_tensors, weight_table, state_codes, rescale):
    sites = site_tensors.shape[0]
    rows = [env_in.shape[1] * part // sum(SPLIT) for part in SPLIT]
    me = lax.axis_index("lbond").astype(jnp.int32).reshape(1)
    terms = [[env_in] for _ in SPLIT]
    table = weight_table.T
    for site in range(sites):
        tiles = load_call(site, devices, me, site_tensors) if PRELOAD and site else None
        for chain in range(len(SPLIT)):
            made = site_call(
                site, sum(rows[:chain]), rows[chain], devices, me, rescale, state_codes, table, terms[chain],
                site_tensors, tiles,
            )
            if tiles is None:
                tiles = made[2]
            terms[chain] = reduce_terms(made[0], made[1], devices)
    factor = rescale[sites - 1].astype(jnp.float32) * 0.5
    outs = []
    for chain in range(len(SPLIT)):
        total = terms[chain][0][0].astype(jnp.float32)
        for term in terms[chain][1:]:
            total = total + term[0].astype(jnp.float32)
        outs.append((total * factor).astype(jnp.bfloat16).T)
    return jnp.concatenate(outs, 1)


def solution(mesh):
    placed = (P("lbond", "groups"), P(None, "lbond", None, None), P(), P(None, "groups"), P())
    devices = mesh.shape["lbond"]
    return jax.shard_map(
        functools.partial(on_device, devices),
        mesh=mesh,
        in_specs=placed,
        out_specs=P("lbond", "groups"),
        check_vma=False,
    )
```
